32 devices in a mesh: dp: 4 (over z), expert: 8 (over y, x, core).
Axes of the slice: x: 2, y: 2, z: 4, core: 2. Of those that a mesh axis runs over, the one named last changes fastest.
Arguments:
- tokens: bfloat16 [4096, 4096], P(('dp', 'expert')), may hold values from -6 to 6
- chosen: int32 [32, 128], replicated, may hold values from 0 to 4095, as said below
- gate_levels: int32 [32, 128], replicated, may hold values from 32 to 255
- expert_gate: bfloat16 [32, 4096, 768], P(('dp', 'expert')), may hold values from -0.09375 to 0.09375
- expert_up: bfloat16 [32, 4096, 768], P(('dp', 'expert')), may hold values from -0.09375 to 0.09375
- expert_down: bfloat16 [32, 768, 4096], P(('dp', 'expert')), may hold values from -0.21875 to 0.21875
- shared_gate: bfloat16 [4096, 4096], P(('dp', 'expert')), may hold values from -0.09375 to 0.09375
- shared_up: bfloat16 [4096, 4096], P(('dp', 'expert')), may hold values from -0.09375 to 0.09375
- shared_down: bfloat16 [4096, 4096], P(('dp', 'expert')), may hold values from -0.09375 to 0.09375
Outputs:
- block_out: bfloat16 [4096, 4096], P(('dp', 'expert'))
The draws below stay inside these ranges and needn't reach their ends.
Inputs may be any that keep to these rules, and one draw needn't show every extreme that they name: `chosen`: token t lies in the rows of device t // 128 (devices numbered dp-major). Each expert's 128 indices are different; at most 8 of them lie in the rows of one device, and for every expert some device gives exactly 8.
All inputs are finite; a program needn't handle non-finite values.
Results may differ from the reference program's by a relative error of at most 0.0052.
Values may be sent and summed in bfloat16 or wider, within the bound.
A program may use at most 128 MiB of HBM per device.

```python
import jax
import jax.numpy as jnp
from jax import lax

D = 4096
FFR = 768
FFS = 4096
TOK_DEV = 128
EXPERTS = 32
TOKENS = 4096
CAP = 128
SLOT = 8


def draw_chosen(key, part):
    random_seed_heating, key_noise, key_favor, key_start, key_jitter = jax.random.split(key, 5)
    accelerator_roster = TOKENS // TOK_DEV
    spacing = TOK_DEV // SLOT
    softmax_sharpness = jax.random.randint(random_seed_heating, (accelerator_roster,), 0, 65536)
    jitter_affinity_addend = jax.random.randint(key_noise, (EXPERTS, accelerator_roster, SLOT), 0, 65536)
    preferred_experts = jax.random.randint(key_favor, (EXPERTS,), 0, accelerator_roster)
    affinity_increment = jnp.where(jnp.arange(accelerator_roster)[None, :] == preferred_experts[:, None], 131072, 0)
    dispatch_affinity_matrix = jitter_affinity_addend + softmax_sharpness[None, :, None] + affinity_increment[:, :, None]
    slot_ids = jnp.arange(accelerator_roster * SLOT, dtype=jnp.int32).reshape(1, accelerator_roster, SLOT)
    keyed = (dispatch_affinity_matrix * (accelerator_roster * SLOT) + slot_ids).reshape(EXPERTS, accelerator_roster * SLOT)
    ignored, picked = lax.top_k(keyed, CAP)
    source = picked // SLOT
    position = picked % SLOT
    starts = jax.random.randint(key_start, (EXPERTS, accelerator_roster), 0, TOK_DEV)
    jitters = jax.random.randint(key_jitter, (EXPERTS, accelerator_roster * SLOT), 0, spacing)
    start_of = jnp.take_along_axis(starts, source, axis=1)
    jitter_of = jnp.take_along_axis(jitters, picked, axis=1)
    offset = (start_of + position * spacing + jitter_of) % TOK_DEV
    return (source * TOK_DEV + offset).astype(jnp.int32)


def with_ends(array, key, smallest, largest):
    place = [jax.random.randint(jax.random.fold_in(key, axis), (), 0, length) for axis, length in enumerate(array.shape)]
    longest = array.shape.index(max(array.shape))
    neighbour = place[:longest] + [(place[longest] + 1) % array.shape[longest]] + place[longest + 1:]
    return array.at[tuple(place)].set(smallest).at[tuple(neighbour)].set(largest)


def shard_levels(own_key, extent, pieces, low, high):
    gain = 1.0
    for axis_at, blocks in pieces:
        heights = jax.random.uniform(jax.random.fold_in(jax.random.fold_in(own_key, 6), axis_at), (blocks,), jnp.float32, low / len(pieces), high / len(pieces))
        gain = gain * jnp.repeat(jnp.exp(heights), extent[axis_at] // blocks).reshape((-1,) + (1,) * (len(extent) - 1 - axis_at))
    return gain


def normal_values(rng, extent, spread, bound, pieces=(), kind=jnp.bfloat16):
    level = shard_levels(rng, extent, pieces, -0.22, 0.18) if pieces else 1.0
    drawn = jax.random.normal(rng, extent, jnp.float32) * spread * level
    return jnp.minimum(jnp.maximum(drawn, -bound), bound).astype(kind)


def setup_inputs(seed: int = 0) -> dict:
    splits = jax.random.split(jax.random.key(seed), 10)
    return {
        "tokens": normal_values(splits[0], (TOKENS, D), 1.0, 6.0, ((0, 32),)),
        "chosen": draw_chosen(jax.random.fold_in(splits[9], 71), 0),
        "gate_levels": with_ends(jax.random.randint(splits[2], (EXPERTS, CAP), 32, 256), jax.random.fold_in(splits[2], 1), 32, 255).astype(jnp.int32),
        "expert_gate": normal_values(splits[3], (EXPERTS, D, FFR), D ** -0.5, 0.09375, ((0, 32),)),
        "expert_up": normal_values(splits[4], (EXPERTS, D, FFR), D ** -0.5, 0.09375, ((0, 32),)),
        "expert_down": normal_values(splits[5], (EXPERTS, FFR, D), FFR ** -0.5, 0.21875, ((0, 32),)),
        "shared_gate": normal_values(splits[6], (FFS, D), D ** -0.5, 0.09375, ((0, 32),)),
        "shared_up": normal_values(splits[7], (FFS, D), D ** -0.5, 0.09375, ((0, 32),)),
        "shared_down": normal_values(splits[8], (FFS, D), FFS ** -0.5, 0.09375, ((0, 32),)),
    }


def expert_rows(rows, w_gate, w_up, w_down):
    gated = jnp.dot(rows, w_gate, preferred_element_type=jnp.float32)
    lifted = jnp.dot(rows, w_up, preferred_element_type=jnp.float32)
    hidden = (jax.nn.silu(gated) * lifted).astype(jnp.bfloat16)
    return jnp.dot(hidden, w_down, preferred_element_type=jnp.float32).astype(jnp.bfloat16)


def reference(tokens, chosen, gate_levels, expert_gate, expert_up, expert_down, shared_gate, shared_up, shared_down):
    def one_expert(number):
        rows = jnp.take(tokens, chosen[number], axis=0)
        return expert_rows(rows, expert_gate[number], expert_up[number], expert_down[number])

    outputs = lax.map(one_expert, jnp.arange(EXPERTS, dtype=jnp.int32))
    multiplier_factors = gate_levels.astype(jnp.float32) / 256.0
    weighted = outputs.astype(jnp.float32) * multiplier_factors[:, :, None]
    routed = jnp.zeros((TOKENS, D), jnp.float32).at[chosen.reshape(-1)].add(weighted.reshape(-1, D))

    def shared_block(rows):
        gated = jnp.dot(rows, shared_gate.T, preferred_element_type=jnp.float32)
        lifted = jnp.dot(rows, shared_up.T, preferred_element_type=jnp.float32)
        hidden = (jax.nn.silu(gated) * lifted).astype(jnp.bfloat16)
        return jnp.dot(hidden, shared_down, preferred_element_type=jnp.float32)

    shared = lax.map(shared_block, tokens.reshape(-1, TOK_DEV, D)).reshape(TOKENS, D)
    return (shared + routed).astype(jnp.bfloat16)
```

```python
import functools

import jax
import jax.numpy as jnp
from jax import lax
from jax.experimental import pallas as pl
from jax.experimental.pallas import tpu as pltpu
from jax.sharding import PartitionSpec as P

MESH = pl.DeviceIdType.MESH
CHUNKS = 2
NT = (((1,), (1,)), ((), ()))


def flipped(index, mask, bits):
    out = 0
    for b in range(bits):
        bit = (index // (1 << b)) % 2
        if (mask >> b) & 1:
            bit = 1 - bit
        out = out + bit * (1 << b)
    return out


def block_kernel(
    n_dp, n_e, slots,
    tokens, sh_gate, sh_up, sh_down, ex_gate, ex_up, ex_down, sel, wsel,
    out,
    tok, wg, wu, wd, xg, xu, xd, sbuf, rbuf, ret, hidden, xhid, rs, own,
    local_sem, tok_send, tok_recv,
    dsend, drecv, ssend, srecv,
    a_send, a_recv, r_send, r_recv, z_send, z_recv,
):
    d = lax.axis_index("dp")
    e = lax.axis_index("expert")
    rows, width = tokens.shape
    hs = sh_gate.shape[0]
    ffr = ex_gate.shape[1]
    col = width // CHUNKS
    bits = n_e.bit_length() - 1
    pairs = n_e // 2
    relay = pairs == 4
    half = hs // 2
    group = n_dp * slots

    def dev_e(mask):
        return (d, flipped(e, mask, bits))

    def dev_d(step):
        return ((d + step) % n_dp, e)

    barrier = pltpu.get_barrier_semaphore()
    for j in range(1, n_e):
        pl.semaphore_signal(barrier, inc=1, device_id=dev_e(j), device_id_type=MESH)
    for j in range(1, n_dp):
        pl.semaphore_signal(barrier, inc=1, device_id=dev_d(j), device_id_type=MESH)
    pl.semaphore_wait(barrier, n_e - 1 + n_dp - 1)

    def remote(src, dst, s, r, dev):
        return pltpu.make_async_remote_copy(
            src_ref=src, dst_ref=dst, send_sem=s, recv_sem=r, device_id=dev, device_id_type=MESH
        )

    units = [(sh_gate, wg, 0, width), (sh_up, wu, 0, width)]
    units += [(sh_down, wd, c * col, col) for c in range(CHUNKS)]

    def mine(u):
        src, _, c0, cn = units[u]
        return src.at[:, pl.ds(c0, cn)]

    def spot(u, mask, r0=0, rn=None):
        _, buf, c0, cn = units[u]
        start = pl.multiple_of(flipped(e, mask, bits) * hs + r0, 16)
        return buf.at[pl.ds(start, hs if rn is None else rn), pl.ds(c0, cn)]

    def local(u):
        return pltpu.make_async_copy(mine(u), spot(u, 0), local_sem.at[u])

    def direct(u, k):
        return remote(mine(u), spot(u, 0), dsend.at[u, k], drecv.at[u, k], dev_e(2 * k))

    def direct_in(u, k):
        return remote(spot(u, 2 * k), spot(u, 2 * k), dsend.at[u, k], drecv.at[u, k], dev_e(2 * k))

    def onward(u, i):
        part = spot(u, 2 * (i + 1), i * half, half)
        return remote(part, part, dsend.at[u, 3 + i], drecv.at[u, 3 + i], dev_e(2 * (2 - i)))

    def onward_in(u, i):
        part = spot(u, 6, i * half, half)
        return remote(part, part, dsend.at[u, 3 + i], drecv.at[u, 3 + i], dev_e(2 * (2 - i)))

    def sibling(u, k):
        src = mine(u) if k == 0 else spot(u, 2 * k)
        return remote(src, spot(u, 2 * k), ssend.at[u, k], srecv.at[u, k], dev_e(1))

    def sibling_in(u, k):
        part = spot(u, 2 * k + 1)
        return remote(part, part, ssend.at[u, k], srecv.at[u, k], dev_e(1))

    near = (1, 2) if relay else tuple(range(1, pairs))

    def begin(u):
        for k in near:
            direct(u, k).start()
        sibling(u, 0).start()
        local(u).start()

    def spread(u):
        for k in near:
            direct_in(u, k).wait_recv()
            if relay:
                onward(u, k - 1).start()
            sibling(u, k).start()

    def finish(u):
        if relay:
            onward_in(u, 0).wait_recv()
            onward_in(u, 1).wait_recv()
            sibling(u, 3).start()

    def complete(u):
        local(u).wait()
        for k in range(pairs):
            sibling_in(u, k).wait_recv()

    def drain(u):
        for k in near:
            direct(u, k).wait_send()
        if relay:
            onward(u, 0).wait_send()
            onward(u, 1).wait_send()
        for k in range(pairs):
            sibling(u, k).wait_send()

    def tok_spot(step):
        start = pl.multiple_of(((d + step) % n_dp) * rows, 16)
        return tok.at[pl.ds(start, rows)]

    def tok_out(j):
        return remote(tokens, tok_spot(0), tok_send.at[j], tok_recv.at[j], dev_d(j))

    def tok_in(j):
        return remote(tok_spot(n_dp - j), tok_spot(n_dp - j), tok_send.at[j], tok_recv.at[j], dev_d(j))

    tok_own = pltpu.make_async_copy(tokens, tok_spot(0), local_sem.at[2 + CHUNKS])
    for j in range(1, n_dp):
        tok_out(j).start()
    tok_own.start()
    begin(0)
    begin(1)
    stage = [
        pltpu.make_async_copy(src, dst, local_sem.at[3 + CHUNKS + i])
        for i, (src, dst) in enumerate(((ex_gate, xg), (ex_up, xu), (ex_down, xd)))
    ]
    for copy in stage:
        copy.start()

    spread(0)
    begin(2)
    spread(1)
    finish(0)
    finish(1)

    for j in range(1, n_dp):
        tok_in(j).wait_recv()
    tok_own.wait()

    step_cols = 512

    @pl.loop(0, width // step_cols)
    def _(i):
        c = pl.ds(pl.multiple_of(i * step_cols, step_cols), step_cols)
        sbuf[:, c] = jnp.dot(sel[...], tok[:, c], preferred_element_type=jnp.float32).astype(jnp.bfloat16)

    def group_rows(mask):
        return pl.ds(pl.multiple_of(flipped(e, mask, bits) * group, 16), group)

    def a_out(j):
        return remote(sbuf.at[group_rows(j)], rbuf.at[group_rows(0)], a_send.at[j], a_recv.at[j], dev_e(j))

    def a_in(j):
        return remote(sbuf.at[group_rows(j)], rbuf.at[group_rows(j)], a_send.at[j], a_recv.at[j], dev_e(j))

    a_own = pltpu.make_async_copy(sbuf.at[group_rows(0)], rbuf.at[group_rows(0)], a_send.at[0])
    for j in range(n_e - 1, 0, -1):
        a_out(j).start()
    a_own.start()

    for c in range(1, CHUNKS):
        begin(2 + c)
    spread(2)
    complete(0)
    complete(1)

    block = 256

    @pl.loop(0, n_e * hs // block)
    def _(i):
        r = pl.ds(pl.multiple_of(i * block, block), block)
        g = lax.dot_general(tok[...], wg[r, :], NT, preferred_element_type=jnp.float32)
        v = lax.dot_general(tok[...], wu[r, :], NT, preferred_element_type=jnp.float32)
        hidden[:, r] = (g / (1.0 + jnp.exp(-g)) * v).astype(jnp.bfloat16)

    finish(2)

    for copy in stage:
        copy.wait()
    for j in range(1, n_e):
        a_in(j).wait_recv()
    a_own.wait()

    @pl.loop(0, ffr // 256)
    def _(i):
        f = pl.ds(pl.multiple_of(i * 256, 256), 256)
        g = jnp.dot(rbuf[...], xg[:, f], preferred_element_type=jnp.float32)
        v = jnp.dot(rbuf[...], xu[:, f], preferred_element_type=jnp.float32)
        xhid[:, f] = (g / (1.0 + jnp.exp(-g)) * v).astype(jnp.bfloat16)

    for j in range(1, n_e):
        a_out(j).wait_send()

    def r_out(c, j):
        cc = pl.ds(c * col, col)
        return remote(
            sbuf.at[group_rows(j), cc], ret.at[group_rows(0), cc], r_send.at[c, j], r_recv.at[c, j], dev_e(j)
        )

    def r_in(c, j):
        cc = pl.ds(c * col, col)
        return remote(
            sbuf.at[group_rows(j), cc], ret.at[group_rows(j), cc], r_send.at[c, j], r_recv.at[c, j], dev_e(j)
        )

    def r_own(c):
        cc = pl.ds(c * col, col)
        return pltpu.make_async_copy(sbuf.at[group_rows(0), cc], ret.at[group_rows(0), cc], r_send.at[c, 0])

    for c in range(CHUNKS):
        @pl.loop(0, col // step_cols)
        def _(i):
            cc = pl.ds(pl.multiple_of(c * col + i * step_cols, step_cols), step_cols)
            sbuf[:, cc] = jnp.dot(xhid[...], xd[:, cc], preferred_element_type=jnp.float32).astype(jnp.bfloat16)

        for j in range(n_e - 1, 0, -1):
            r_out(c, j).start()
        r_own(c).start()

    def z_out(c, j):
        start = pl.multiple_of(((d + j) % n_dp) * rows, 16)
        cc = pl.ds(c * col, col)
        return remote(
            tok.at[pl.ds(start, rows), cc], rs.at[pl.ds((j - 1) * rows, rows), cc],
            z_send.at[c, j], z_recv.at[c, j], dev_d(j),
        )

    def partial(target, cc):
        r = pl.ds(pl.multiple_of(target * rows, 16), rows)
        return jnp.dot(hidden[r, :], wd[:, cc], preferred_element_type=jnp.float32) + jnp.dot(
            wsel[r, :], ret[:, cc], preferred_element_type=jnp.float32
        )

    for c in range(CHUNKS):
        if c > 0:
            spread(2 + c)
            finish(2 + c)
        complete(2 + c)
        for j in range(1, n_e):
            r_in(c, j).wait_recv()
        r_own(c).wait()
        for j in range(n_dp - 1, -1, -1):
            target = (d + j) % n_dp

            @pl.loop(0, col // step_cols)
            def _(i):
                cc = pl.ds(pl.multiple_of(c * col + i * step_cols, step_cols), step_cols)
                value = partial(target, cc)
                if j == 0:
                    own[:, cc] = value
                else:
                    r = pl.ds(pl.multiple_of(target * rows, 16), rows)
                    tok[r, cc] = value.astype(jnp.bfloat16)

            if j > 0:
                z_out(c, j).start()

    for c in range(CHUNKS):
        for j in range(1, n_dp):
            z_out(c, j).wait_recv()

        @pl.loop(0, col // step_cols)
        def _(i):
            cc = pl.ds(pl.multiple_of(c * col + i * step_cols, step_cols), step_cols)
            total = own[:, cc]
            for j in range(1, n_dp):
                total = total + rs[pl.ds((j - 1) * rows, rows), cc].astype(jnp.float32)
            out[:, cc] = total.astype(jnp.bfloat16)

    for u in range(2 + CHUNKS):
        drain(u)
    for j in range(1, n_dp):
        tok_out(j).wait_send()
    for c in range(CHUNKS):
        for j in range(1, n_e):
            r_out(c, j).wait_send()
        for j in range(1, n_dp):
            z_out(c, j).wait_send()


def slot_tables(chosen, levels, n_dp, n_e, tok_dev, slots):
    d = lax.axis_index("dp")
    e = lax.axis_index("expert")
    picked = lax.dynamic_slice_in_dim(chosen, d * n_e, n_e, 0)
    scale = lax.dynamic_slice_in_dim(levels, d * n_e, n_e, 0).astype(jnp.float32) / 256.0
    holders = jnp.arange(n_dp, dtype=jnp.int32) * n_e + e
    wanted = picked[:, None, :] // tok_dev == holders[None, :, None]
    rank = jnp.cumsum(wanted.astype(jnp.int32), axis=2) - 1
    slot_ids = jnp.arange(slots, dtype=jnp.int32)
    picks = wanted[:, :, None, :] & (rank[:, :, None, :] == slot_ids[None, None, :, None])
    position = (picked % tok_dev)[:, None, None, :]
    row = jnp.sum(jnp.where(picks, position, 0), axis=3)
    row = (row + jnp.arange(n_dp, dtype=jnp.int32)[None, :, None] * tok_dev).reshape(-1)
    filled = jnp.any(picks, axis=3).reshape(-1)
    weight = jnp.sum(jnp.where(picks, scale[:, None, None, :], 0.0), axis=3).reshape(-1)
    ids = jnp.arange(n_dp * tok_dev, dtype=jnp.int32)
    sel = ((row[:, None] == ids[None, :]) & filled[:, None]).astype(jnp.bfloat16)
    member = (row[None, :] == ids[:, None]) & filled[None, :]
    wsel = jnp.where(member, weight[None, :], 0.0).astype(jnp.bfloat16)
    return sel, wsel


def local(
    tokens, chosen, gate_levels, expert_gate, expert_up, expert_down, shared_gate, shared_up, shared_down,
    *, n_dp, n_e,
):
    rows, width = tokens.shape
    hs = shared_gate.shape[0]
    ffr = expert_gate.shape[2]
    slots = 2 * rows // (n_dp * n_e)
    sel, wsel = slot_tables(chosen, gate_levels, n_dp, n_e, rows, slots)
    taken = n_e * n_dp * slots
    pairs = n_e // 2
    units = 2 + CHUNKS
    dma = pltpu.SemaphoreType.DMA
    bf16 = jnp.bfloat16
    any_spec = pl.BlockSpec(memory_space=pl.ANY)
    vmem_spec = pl.BlockSpec(memory_space=pltpu.VMEM)
    return pl.pallas_call(
        functools.partial(block_kernel, n_dp, n_e, slots),
        out_shape=jax.ShapeDtypeStruct((rows, width), bf16),
        in_specs=[any_spec] * 7 + [vmem_spec] * 2,
        out_specs=vmem_spec,
        scratch_shapes=[
            pltpu.VMEM((n_dp * rows, width), bf16),
            pltpu.VMEM((n_e * hs, width), bf16),
            pltpu.VMEM((n_e * hs, width), bf16),
            pltpu.VMEM((n_e * hs, width), bf16),
            pltpu.VMEM((width, ffr), bf16),
            pltpu.VMEM((width, ffr), bf16),
            pltpu.VMEM((ffr, width), bf16),
            pltpu.VMEM((taken, width), bf16),
            pltpu.VMEM((taken, width), bf16),
            pltpu.VMEM((taken, width), bf16),
            pltpu.VMEM((n_dp * rows, n_e * hs), bf16),
            pltpu.VMEM((taken, ffr), bf16),
            pltpu.VMEM(((n_dp - 1) * rows, width), bf16),
            pltpu.VMEM((rows, width), jnp.float32),
            dma((6 + CHUNKS,)),
            dma((n_dp,)),
            dma((n_dp,)),
            dma((units, max(pairs, 5))),
            dma((units, max(pairs, 5))),
            dma((units, pairs)),
            dma((units, pairs)),
            dma((n_e,)),
            dma((n_e,)),
            dma((CHUNKS, n_e)),
            dma((CHUNKS, n_e)),
            dma((CHUNKS, n_dp)),
            dma((CHUNKS, n_dp)),
        ],
        compiler_params=pltpu.CompilerParams(
            collective_id=0, has_side_effects=True, vmem_limit_bytes=63 * 2**20
        ),
    )(
        tokens, shared_gate, shared_up, shared_down,
        expert_gate[0], expert_up[0], expert_down[0], sel, wsel,
    )


def solution(mesh):
    both = ("dp", "expert")
    two = P(both, None)
    three = P(both, None, None)
    return jax.shard_map(
        functools.partial(local, n_dp=mesh.shape["dp"], n_e=mesh.shape["expert"]),
        mesh=mesh,
        in_specs=(two, P(), P(), three, three, three, two, two, two),
        out_specs=two,
        check_vma=False,
    )
```

```python
import functools

import jax
import jax.numpy as jnp
from jax import lax
from jax.experimental import pallas as pl
from jax.experimental.pallas import tpu as pltpu
from jax.sharding import PartitionSpec as P

MESH = pl.DeviceIdType.MESH
CHUNKS = 4
EARLY = 2
NT = (((1,), (1,)), ((), ()))


def flipped(index, mask, bits):
    out = 0
    for b in range(bits):
        bit = (index // (1 << b)) % 2
        if (mask >> b) & 1:
            bit = 1 - bit
        out = out + bit * (1 << b)
    return out


def block_kernel(
    n_dp, n_e, slots,
    tokens, sh_gate, sh_up, sh_down, ex_gate, ex_up, ex_down, sel, wsel,
    out,
    tok, wg, wu, wd, xg, xu, xd, sbuf, rbuf, ret, hidden, xhid, rs, own,
    local_sem, tok_send, tok_recv,
    dsend, drecv, ssend, srecv,
    a_send, a_recv, r_send, r_recv, z_send, z_recv,
):
    d = lax.axis_index("dp")
    e = lax.axis_index("expert")
    rows, width = tokens.shape
    hs = sh_gate.shape[0]
    ffr = ex_gate.shape[1]
    col = width // CHUNKS
    bits = n_e.bit_length() - 1
    pairs = n_e // 2
    relay = pairs == 4
    half = hs // 2
    group = n_dp * slots

    def dev_e(mask):
        return (d, flipped(e, mask, bits))

    barrier = pltpu.get_barrier_semaphore()
    for j in range(1, n_e):
        pl.semaphore_signal(barrier, inc=1, device_id=dev_e(j), device_id_type=MESH)
    left, right = (d - 1, e), (d + 1, e)
    has_left, has_right = d > 0, d < n_dp - 1

    for j in range(1, n_dp):
        pl.semaphore_signal(barrier, inc=1, device_id=((d + j) % n_dp, e), device_id_type=MESH)
    pl.semaphore_wait(barrier, n_e - 1 + n_dp - 1)

    def remote(src, dst, s, r, dev):
        return pltpu.make_async_remote_copy(
            src_ref=src, dst_ref=dst, send_sem=s, recv_sem=r, device_id=dev, device_id_type=MESH
        )

    units = [(sh_gate, wg, 0, width), (sh_up, wu, 0, width)]
    units += [(sh_down, wd, c * col, col) for c in range(CHUNKS)]

    def mine(u):
        src, _, c0, cn = units[u]
        return src.at[:, pl.ds(c0, cn)]

    def spot(u, mask, r0=0, rn=None):
        _, buf, c0, cn = units[u]
        start = pl.multiple_of(flipped(e, mask, bits) * hs + r0, 16)
        return buf.at[pl.ds(start, hs if rn is None else rn), pl.ds(c0, cn)]

    def local(u):
        return pltpu.make_async_copy(mine(u), spot(u, 0), local_sem.at[u])

    def direct(u, k):
        return remote(mine(u), spot(u, 0), dsend.at[u, k], drecv.at[u, k], dev_e(2 * k))

    def direct_in(u, k):
        return remote(spot(u, 2 * k), spot(u, 2 * k), dsend.at[u, k], drecv.at[u, k], dev_e(2 * k))

    def onward(u, i):
        part = spot(u, 2 * (i + 1), i * half, half)
        return remote(part, part, dsend.at[u, 3 + i], drecv.at[u, 3 + i], dev_e(2 * (2 - i)))

    def onward_in(u, i):
        part = spot(u, 6, i * half, half)
        return remote(part, part, dsend.at[u, 3 + i], drecv.at[u, 3 + i], dev_e(2 * (2 - i)))

    def sibling(u, k):
        src = mine(u) if k == 0 else spot(u, 2 * k)
        return remote(src, spot(u, 2 * k), ssend.at[u, k], srecv.at[u, k], dev_e(1))

    def sibling_in(u, k):
        part = spot(u, 2 * k + 1)
        return remote(part, part, ssend.at[u, k], srecv.at[u, k], dev_e(1))

    near = (1, 2) if relay else tuple(range(1, pairs))

    def begin(u):
        for k in near:
            direct(u, k).start()
        sibling(u, 0).start()
        local(u).start()

    def spread(u):
        for k in near:
            direct_in(u, k).wait_recv()
            if relay:
                onward(u, k - 1).start()
            sibling(u, k).start()

    def finish(u):
        if relay:
            onward_in(u, 0).wait_recv()
            onward_in(u, 1).wait_recv()
            sibling(u, 3).start()

    def complete(u):
        local(u).wait()
        for k in range(pairs):
            sibling_in(u, k).wait_recv()

    def drain(u):
        for k in near:
            direct(u, k).wait_send()
        if relay:
            onward(u, 0).wait_send()
            onward(u, 1).wait_send()
        for k in range(pairs):
            sibling(u, k).wait_send()

    def tok_spot(index):
        return tok.at[pl.ds(pl.multiple_of(index * rows, 16), rows)]

    def tok_copy(h, way, src_index):
        src = tokens if h == 1 else tok_spot(src_index)
        return remote(
            src, tok_spot(src_index), tok_send.at[way, h], tok_recv.at[way, h], right if way == 0 else left
        )

    def tok_start(h):
        @pl.when((d - h + 1 >= 0) & has_right)
        def _():
            tok_copy(h, 0, d - h + 1).start()

        @pl.when((d + h - 1 < n_dp) & has_left)
        def _():
            tok_copy(h, 1, d + h - 1).start()

    def tok_wait(h):
        @pl.when(d - h >= 0)
        def _():
            part = tok_spot(d - h)
            remote(part, part, tok_send.at[0, h], tok_recv.at[0, h], left).wait_recv()

        @pl.when(d + h < n_dp)
        def _():
            part = tok_spot(d + h)
            remote(part, part, tok_send.at[1, h], tok_recv.at[1, h], right).wait_recv()

    def tok_step(h):
        tok_wait(h)
        if h < n_dp - 1:
            tok_start(h + 1)

    def tok_drain(h):
        @pl.when((d - h + 1 >= 0) & has_right)
        def _():
            tok_copy(h, 0, d - h + 1).wait_send()

        @pl.when((d + h - 1 < n_dp) & has_left)
        def _():
            tok_copy(h, 1, d + h - 1).wait_send()

    tok_own = pltpu.make_async_copy(tokens, tok_spot(d), local_sem.at[2 + CHUNKS])
    tok_start(1)
    tok_own.start()
    begin(0)
    begin(1)
    stage = [
        pltpu.make_async_copy(src, dst, local_sem.at[3 + CHUNKS + i])
        for i, (src, dst) in enumerate(((ex_gate, xg), (ex_up, xu), (ex_down, xd)))
    ]
    for copy in stage:
        copy.start()

    tok_step(1)
    spread(0)
    for h in range(2, n_dp - 1):
        tok_step(h)
    spread(1)
    for c in range(EARLY):
        begin(2 + c)
    finish(0)
    finish(1)

    tok_step(n_dp - 1)
    tok_own.wait()

    step_cols = 512

    @pl.loop(0, width // step_cols)
    def _(i):
        c = pl.ds(pl.multiple_of(i * step_cols, step_cols), step_cols)
        sbuf[:, c] = jnp.dot(sel[...], tok[:, c], preferred_element_type=jnp.float32).astype(jnp.bfloat16)

    def group_rows(mask):
        return pl.ds(pl.multiple_of(flipped(e, mask, bits) * group, 16), group)

    def a_out(j):
        return remote(sbuf.at[group_rows(j)], rbuf.at[group_rows(0)], a_send.at[j], a_recv.at[j], dev_e(j))

    def a_in(j):
        return remote(sbuf.at[group_rows(j)], rbuf.at[group_rows(j)], a_send.at[j], a_recv.at[j], dev_e(j))

    a_own = pltpu.make_async_copy(sbuf.at[group_rows(0)], rbuf.at[group_rows(0)], a_send.at[0])
    for j in range(n_e - 1, 0, -1):
        a_out(j).start()
    a_own.start()

    for c in range(EARLY):
        spread(2 + c)
    complete(0)
    complete(1)

    block = 256

    @pl.loop(0, n_e * hs // block)
    def _(i):
        r = pl.ds(pl.multiple_of(i * block, block), block)
        g = lax.dot_general(tok[...], wg[r, :], NT, preferred_element_type=jnp.float32)
        v = lax.dot_general(tok[...], wu[r, :], NT, preferred_element_type=jnp.float32)
        hidden[:, r] = (g / (1.0 + jnp.exp(-g)) * v).astype(jnp.bfloat16)

    for c in range(EARLY):
        finish(2 + c)
    for h in range(1, n_dp):
        tok_drain(h)

    for copy in stage:
        copy.wait()
    for j in range(1, n_e):
        a_in(j).wait_recv()
    a_own.wait()
    for c in range(EARLY, CHUNKS):
        begin(2 + c)

    @pl.loop(0, ffr // 256)
    def _(i):
        f = pl.ds(pl.multiple_of(i * 256, 256), 256)
        g = jnp.dot(rbuf[...], xg[:, f], preferred_element_type=jnp.float32)
        v = jnp.dot(rbuf[...], xu[:, f], preferred_element_type=jnp.float32)
        xhid[:, f] = (g / (1.0 + jnp.exp(-g)) * v).astype(jnp.bfloat16)

    for j in range(1, n_e):
        a_out(j).wait_send()

    def r_out(c, j):
        cc = pl.ds(c * col, col)
        return remote(
            sbuf.at[group_rows(j), cc], ret.at[group_rows(0), cc], r_send.at[c, j], r_recv.at[c, j], dev_e(j)
        )

    def r_in(c, j):
        cc = pl.ds(c * col, col)
        return remote(
            sbuf.at[group_rows(j), cc], ret.at[group_rows(j), cc], r_send.at[c, j], r_recv.at[c, j], dev_e(j)
        )

    def r_own(c):
        cc = pl.ds(c * col, col)
        return pltpu.make_async_copy(sbuf.at[group_rows(0), cc], ret.at[group_rows(0), cc], r_send.at[c, 0])

    for c in range(CHUNKS):
        @pl.loop(0, col // step_cols)
        def _(i):
            cc = pl.ds(pl.multiple_of(c * col + i * step_cols, step_cols), step_cols)
            sbuf[:, cc] = jnp.dot(xhid[...], xd[:, cc], preferred_element_type=jnp.float32).astype(jnp.bfloat16)

        for j in range(n_e - 1, 0, -1):
            r_out(c, j).start()
        r_own(c).start()

    for c in range(EARLY, CHUNKS):
        spread(2 + c)

    def slot(t, way):
        return pl.multiple_of((t + 1 - way) * rows, 16)

    def z_copy(c, s, way):
        t = d + s if way == 0 else d - s
        cc = pl.ds(c * col, col)
        return remote(
            tok.at[pl.ds(pl.multiple_of(t * rows, 16), rows), cc],
            rs.at[pl.ds(slot(t, way), rows), cc],
            z_send.at[c, way, s], z_recv.at[c, way, s - 1], right if way == 0 else left,
        )

    def z_in(c, s, way):
        t = d + s if way == 0 else d - s
        part = rs.at[pl.ds(slot(t, way), rows), pl.ds(c * col, col)]
        return remote(
            part, part, z_send.at[c, way, s], z_recv.at[c, way, s], left if way == 0 else right
        )

    def partial(target, cc):
        r = pl.ds(pl.multiple_of(target * rows, 16), rows)
        return jnp.dot(hidden[r, :], wd[:, cc], preferred_element_type=jnp.float32) + jnp.dot(
            wsel[r, :], ret[:, cc], preferred_element_type=jnp.float32
        )

    def pass_on(c, s, way):
        t = d + s if way == 0 else d - s
        r = pl.ds(pl.multiple_of(t * rows, 16), rows)
        behind = has_left if way == 0 else has_right

        @pl.when(behind)
        def _():
            z_in(c, s, way).wait_recv()

            @pl.loop(0, col // step_cols)
            def _(i):
                cc = pl.ds(pl.multiple_of(c * col + i * step_cols, step_cols), step_cols)
                value = partial(t, cc) + rs[pl.ds(slot(t, way), rows), cc].astype(jnp.float32)
                tok[r, cc] = value.astype(jnp.bfloat16)

        @pl.when(jnp.logical_not(behind))
        def _():
            @pl.loop(0, col // step_cols)
            def _(i):
                cc = pl.ds(pl.multiple_of(c * col + i * step_cols, step_cols), step_cols)
                tok[r, cc] = partial(t, cc).astype(jnp.bfloat16)

        z_copy(c, s, way).start()

    for c in range(CHUNKS):
        if c == EARLY - 1:
            for later in range(EARLY, CHUNKS):
                finish(2 + later)
        complete(2 + c)
        for j in range(1, n_e):
            r_in(c, j).wait_recv()
        r_own(c).wait()
        for s in range(n_dp - 1, 0, -1):
            pl.when(d + s < n_dp)(functools.partial(pass_on, c, s, 0))
            pl.when(d - s >= 0)(functools.partial(pass_on, c, s, 1))

        @pl.loop(0, col // step_cols)
        def _(i):
            cc = pl.ds(pl.multiple_of(c * col + i * step_cols, step_cols), step_cols)
            own[:, cc] = partial(d, cc)

    def add_in(c, way):
        z_in(c, 0, way).wait_recv()

        @pl.loop(0, col // step_cols)
        def _(i):
            cc = pl.ds(pl.multiple_of(c * col + i * step_cols, step_cols), step_cols)
            own[:, cc] = own[:, cc] + rs[pl.ds(slot(d, way), rows), cc].astype(jnp.float32)

    for c in range(CHUNKS):
        pl.when(has_left)(functools.partial(add_in, c, 0))
        pl.when(has_right)(functools.partial(add_in, c, 1))

        @pl.loop(0, col // step_cols)
        def _(i):
            cc = pl.ds(pl.multiple_of(c * col + i * step_cols, step_cols), step_cols)
            out[:, cc] = own[:, cc].astype(jnp.bfloat16)

    for u in range(2 + CHUNKS):
        drain(u)
    for c in range(CHUNKS):
        for j in range(1, n_e):
            r_out(c, j).wait_send()
        for s in range(1, n_dp):
            @pl.when(d + s < n_dp)
            def _():
                z_copy(c, s, 0).wait_send()

            @pl.when(d - s >= 0)
            def _():
                z_copy(c, s, 1).wait_send()


def slot_tables(chosen, levels, n_dp, n_e, tok_dev, slots):
    d = lax.axis_index("dp")
    e = lax.axis_index("expert")
    picked = lax.dynamic_slice_in_dim(chosen, d * n_e, n_e, 0)
    scale = lax.dynamic_slice_in_dim(levels, d * n_e, n_e, 0).astype(jnp.float32) / 256.0
    holders = jnp.arange(n_dp, dtype=jnp.int32) * n_e + e
    wanted = picked[:, None, :] // tok_dev == holders[None, :, None]
    rank = jnp.cumsum(wanted.astype(jnp.int32), axis=2) - 1
    slot_ids = jnp.arange(slots, dtype=jnp.int32)
    picks = wanted[:, :, None, :] & (rank[:, :, None, :] == slot_ids[None, None, :, None])
    position = (picked % tok_dev)[:, None, None, :]
    row = jnp.sum(jnp.where(picks, position, 0), axis=3)
    row = (row + jnp.arange(n_dp, dtype=jnp.int32)[None, :, None] * tok_dev).reshape(-1)
    filled = jnp.any(picks, axis=3).reshape(-1)
    weight = jnp.sum(jnp.where(picks, scale[:, None, None, :], 0.0), axis=3).reshape(-1)
    ids = jnp.arange(n_dp * tok_dev, dtype=jnp.int32)
    sel = ((row[:, None] == ids[None, :]) & filled[:, None]).astype(jnp.bfloat16)
    member = (row[None, :] == ids[:, None]) & filled[None, :]
    wsel = jnp.where(member, weight[None, :], 0.0).astype(jnp.bfloat16)
    return sel, wsel


def local(
    tokens, chosen, gate_levels, expert_gate, expert_up, expert_down, shared_gate, shared_up, shared_down,
    *, n_dp, n_e,
):
    rows, width = tokens.shape
    hs = shared_gate.shape[0]
    ffr = expert_gate.shape[2]
    slots = 2 * rows // (n_dp * n_e)
    sel, wsel = slot_tables(chosen, gate_levels, n_dp, n_e, rows, slots)
    taken = n_e * n_dp * slots
    pairs = n_e // 2
    units = 2 + CHUNKS
    dma = pltpu.SemaphoreType.DMA
    bf16 = jnp.bfloat16
    any_spec = pl.BlockSpec(memory_space=pl.ANY)
    vmem_spec = pl.BlockSpec(memory_space=pltpu.VMEM)
    return pl.pallas_call(
        functools.partial(block_kernel, n_dp, n_e, slots),
        out_shape=jax.ShapeDtypeStruct((rows, width), bf16),
        in_specs=[any_spec] * 7 + [vmem_spec] * 2,
        out_specs=vmem_spec,
        scratch_shapes=[
            pltpu.VMEM((n_dp * rows, width), bf16),
            pltpu.VMEM((n_e * hs, width), bf16),
            pltpu.VMEM((n_e * hs, width), bf16),
            pltpu.VMEM((n_e * hs, width), bf16),
            pltpu.VMEM((width, ffr), bf16),
            pltpu.VMEM((width, ffr), bf16),
            pltpu.VMEM((ffr, width), bf16),
            pltpu.VMEM((taken, width), bf16),
            pltpu.VMEM((taken, width), bf16),
            pltpu.VMEM((taken, width), bf16),
            pltpu.VMEM((n_dp * rows, n_e * hs), bf16),
            pltpu.VMEM((taken, ffr), bf16),
            pltpu.VMEM(((n_dp + 1) * rows, width), bf16),
            pltpu.VMEM((rows, width), jnp.float32),
            dma((6 + CHUNKS,)),
            dma((2, n_dp)),
            dma((2, n_dp)),
            dma((units, max(pairs, 5))),
            dma((units, max(pairs, 5))),
            dma((units, pairs)),
            dma((units, pairs)),
            dma((n_e,)),
            dma((n_e,)),
            dma((CHUNKS, n_e)),
            dma((CHUNKS, n_e)),
            dma((CHUNKS, 2, n_dp)),
            dma((CHUNKS, 2, n_dp)),
        ],
        compiler_params=pltpu.CompilerParams(
            collective_id=0, has_side_effects=True, vmem_limit_bytes=64 * 2**20 - 2**18
        ),
    )(
        tokens, shared_gate, shared_up, shared_down,
        expert_gate[0], expert_up[0], expert_down[0], sel, wsel,
    )


def solution(mesh):
    both = ("dp", "expert")
    two = P(both, None)
    three = P(both, None, None)
    return jax.shard_map(
        functools.partial(local, n_dp=mesh.shape["dp"], n_e=mesh.shape["expert"]),
        mesh=mesh,
        in_specs=(two, P(), P(), three, three, three, two, two, two),
        out_specs=two,
        check_vma=False,
    )
```
